32 devices in a mesh: grid: 2 (over core), pts: 16 (over z, y, x).
Axes of the slice: x: 2, y: 2, z: 4, core: 2. Of those that a mesh axis runs over, the one named last changes fastest.
Arguments:
- spectrum: float32 [2, 7168, 1152], P('grid', 'pts'), may hold values from 0.1 to 1
- interaction: bfloat16 [1152, 1152], replicated, may hold values from -0.1875 to 0.1875
- comp_speed: float32 [2, 1152], replicated, may hold values from -0.45 to 0.45
- sea_mask: int32 [2, 7168], replicated, may hold values 0 or 1
- stokes_kernel: float32 [1152, 80], replicated, may hold values from -0.1875 to 0.1875
- tile_owner: int32 [2, 7168, 1], P('grid', 'pts'), may hold values from 0 to 15; in each aligned block of 448 rows (0 to 447, 448 to 895, ..., all dimensions but the last counted through in order) at most 56 rows name the same one
- ocean_column: int32 [2, 7168], P('grid', 'pts'), may hold values from 0 to 255
- neighbours: int32 [2, 4096, 4], P('grid', 'pts'), may hold values from 0 to 255
- coriolis: float32 [2, 4096], P('grid', 'pts'), may hold values from -1 to 1
- velocity: float32 [2, 2, 40, 4096], P('grid', None, None, 'pts'), may hold values from -6 to 6
Outputs:
- spectrum_next: float32 [2, 7168, 1152], P('grid', 'pts')
- velocity_next: float32 [2, 2, 40, 4096], P('grid', None, None, 'pts')
The draws below stay inside these ranges and needn't reach their ends.
Inputs may be any that keep to these rules, and one draw needn't show every extreme that they name: `tile_owner`: at most 56 of the rows of one device name the same tile, and some tile takes exactly 56 of them.
All inputs are finite; a program needn't handle non-finite values.
Results may differ from the reference program's by a relative error of at most 0.0003.
Values sent between devices are 32-bit elements; how exact they have to be, the bound alone decides.
No kernel may reach another device: no remote copies, remote signals or barrier semaphores. Data moves between devices by JAX's collectives and lax.ppermute only.
A program may use at most 128 MiB of HBM per device.

```python
import math
import jax
import jax.numpy as jnp
import numpy as np
from jax import lax

K = 1152
PTS_DEV = 448
GC = 256
LEVELS = 40
COLS = 256
SUBSTEPS = 4
P_SIZE = 7168
CAP = 56
TILES = 4096
N_PTS = 16


def touch_ends(entries, own_key, least, high):
    index_at = [jax.random.randint(jax.random.fold_in(own_key, axis), (), 0, length) for axis, length in enumerate(entries.shape)]
    longest = entries.shape.index(max(entries.shape))
    next_to = index_at[:longest] + [(index_at[longest] + 1) % entries.shape[longest]] + index_at[longest + 1:]
    return entries.at[tuple(index_at)].set(least).at[tuple(next_to)].set(high)


def level_of(rng, shape, cuts, low, top_value):
    def one(axis_at, shards_of):
        heights = jax.random.uniform(jax.random.fold_in(jax.random.fold_in(rng, 6), axis_at), (shards_of,), jnp.float32, low / len(cuts), top_value / len(cuts))
        return jnp.repeat(jnp.exp(heights), shape[axis_at] // shards_of).reshape((-1,) + (1,) * (len(shape) - axis_at - 1))

    gain = one(*cuts[0])
    for cut in cuts[1:]:
        gain = gain * one(*cut)
    return gain


def deal_out(stream_key, own, number, rows, amount, top, most, lean):
    sequence = jax.random.permutation(stream_key, amount)
    packed, usual = portions_of(amount, rows * top, most, lean, True), portions_of(amount, rows * top, most, lean, False)
    places = jnp.arange(amount)

    def named(lengths, rotation):
        used = int((lengths > 0).sum())
        fixed = max(1, used // 4)
        passed = fixed + (places - fixed + rotation * (used - fixed)) % max(1, amount - fixed)
        return jnp.zeros((amount,), jnp.int32).at[sequence[jnp.where(places < fixed, places, passed)]].set(jnp.asarray(lengths, jnp.int32))

    lengths = jnp.where(number % 4 == 0, named(packed, number // 4), named(usual, number - number // 4 - 1))
    mixed = jax.random.permutation(jax.random.fold_in(own, 3), amount)
    giver, taker = mixed[0:amount // 2 * 2:2], mixed[1:amount // 2 * 2:2]
    slack = jnp.minimum(lengths[giver] - 1, most - lengths[taker]) // 2
    slack = jnp.where((giver == sequence[0]) | (taker == sequence[0]) | (lengths[taker] == 0), 0, jnp.maximum(slack, 0))
    passed = jax.random.randint(jax.random.fold_in(own, 4), (amount // 2,), 0, 1 << 20) % (slack + 1)
    lengths = lengths.at[giver].add(-passed).at[taker].add(passed)
    labels = jnp.searchsorted(jnp.cumsum(lengths), jnp.arange(rows * top), side="right").astype(jnp.int32)
    grid = labels.reshape(top, rows).T
    grid = grid[jax.random.permutation(jax.random.fold_in(own, 1), rows)]
    rotation = jax.random.randint(jax.random.fold_in(own, 2), (rows, 1), 0, top)
    return jnp.take_along_axis(grid, (jnp.arange(top)[None, :] + rotation) % top, axis=1)


def portions_of(number_of, total, reach, skew, full):
    loads = [(1 << 20) // math.isqrt(grade ** skew) + 1 for grade in range(1, number_of + 1)]
    largest = reach if full else min(reach, max(-(-total // number_of), total * loads[0] // sum(loads)))
    least = 1 if total - largest >= number_of - 1 else 0
    holding, rest = [largest] + [least] * (number_of - 1), total - largest - least * (number_of - 1)
    while rest > 0:
        candidates = [i for i in range(1, number_of) if holding[i] < largest] or [i for i in range(1, number_of) if holding[i] < reach]
        whole, left = sum([loads[i] for i in candidates]), rest
        for i in candidates:
            more = min(reach - holding[i], max(1, left * loads[i] // whole), rest)
            holding[i] = holding[i] + more
            rest = rest - more
    return np.array(holding)


def centred(stream_key, dims, scale, bound, shards=(), kind=jnp.bfloat16):
    gain = level_of(stream_key, dims, shards, -0.22, 0.18) if shards else 1.0
    array = jax.random.normal(stream_key, dims, jnp.float32) * scale * gain
    return jnp.minimum(jnp.maximum(array, -bound), bound).astype(kind)


def setup_inputs(seed: int = 0) -> dict:
    arg_keys = jax.random.split(jax.random.key(seed), 11)
    spectrum = jnp.clip(jnp.exp(math.log(1.0) - 2.3025851 * jax.random.uniform(arg_keys[0], (2, P_SIZE, K), jnp.float32) ** level_of(arg_keys[0], (2, P_SIZE, K), ((0, 2), (1, 16)), -0.2, 0.2)), 0.1, 1.0)
    interaction = centred(arg_keys[1], (K, K), K ** -0.5, 0.1875)
    comp_speed = jnp.clip(jax.random.uniform(arg_keys[2], (2, K), jnp.float32, -0.45, 0.45), -0.45, 0.45)
    sea_mask = touch_ends((jax.random.randint(arg_keys[3], (2, P_SIZE), 0, 5) < 4).astype(jnp.int32), jax.random.fold_in(arg_keys[3], 1), 0, 1)
    stokes_kernel = centred(arg_keys[4], (K, 2 * LEVELS), K ** -0.5, 0.1875, (), jnp.float32)
    tile_owner_keys = jax.random.split(jax.random.fold_in(arg_keys[5], 1), 2 * P_SIZE // PTS_DEV)
    tile_owner_turns = jax.random.permutation(jax.random.fold_in(arg_keys[5], 3), 2 * P_SIZE // PTS_DEV)
    tile_owner = jax.vmap(lambda own, number: deal_out(jax.random.fold_in(arg_keys[5], 2), own, number, PTS_DEV, N_PTS, 1, CAP, 2))(tile_owner_keys, tile_owner_turns).reshape((2, P_SIZE, 1))
    ocean_column = touch_ends(jax.random.randint(arg_keys[6], (2, P_SIZE), 0, COLS), jax.random.fold_in(arg_keys[6], 1), 0, COLS - 1).astype(jnp.int32)
    neighbours = touch_ends(jax.random.randint(arg_keys[7], (2, TILES, 4), 0, COLS), jax.random.fold_in(arg_keys[7], 1), 0, COLS - 1).astype(jnp.int32)
    coriolis = jnp.clip(jax.random.uniform(arg_keys[8], (2, TILES), jnp.float32, -1.0, 1.0) * level_of(arg_keys[8], (2, TILES), ((0, 2), (1, 16)), -0.4, 0.0), -1.0, 1.0)
    velocity = centred(arg_keys[9], (2, 2, LEVELS, TILES), 1.0, 6.0, ((0, 2), (3, 16)), jnp.float32)
    return {"spectrum": spectrum, "interaction": interaction, "comp_speed": comp_speed, "sea_mask": sea_mask, "stokes_kernel": stokes_kernel, "tile_owner": tile_owner, "ocean_column": ocean_column, "neighbours": neighbours, "coriolis": coriolis, "velocity": velocity}


def advect(field, speed_x, speed_y, mask, top, bottom):
    upper = jnp.concatenate([top[:, None, :], field[:, :-1]], axis=1)
    lower = jnp.concatenate([field[:, 1:], bottom[:, None, :]], axis=1)
    zeros = jnp.zeros_like(field[:, :, :1])
    left = jnp.concatenate([zeros, field[:, :, :-1]], axis=2)
    right = jnp.concatenate([field[:, :, 1:], zeros], axis=2)
    sx = speed_x[:, None, None]
    sy = speed_y[:, None, None]
    result = field - jnp.maximum(sx, 0.0) * (field - upper) - jnp.minimum(sx, 0.0) * (lower - field)
    result = result - jnp.maximum(sy, 0.0) * (field - left) - jnp.minimum(sy, 0.0) * (right - field)
    return result * mask


def reference(spectrum, interaction, comp_speed, sea_mask, stokes_kernel, tile_owner, ocean_column, neighbours, coriolis, velocity):
    points = spectrum.shape[1]
    comps = spectrum.shape[2]
    rows = points // GC
    held = points // N_PTS
    flat = spectrum.reshape(2 * points, comps)
    mix = jnp.dot(flat.astype(jnp.bfloat16), interaction, preferred_element_type=jnp.float32)
    relaxed = (flat + 0.5 * flat * jnp.tanh(mix)).reshape(2, N_PTS, held, comps)
    placed = jnp.transpose(relaxed, (0, 2, 1, 3)).reshape(2 * points, comps)
    stacked = placed.T.reshape(N_PTS, comps // N_PTS, 2 * rows, GC)
    speeds = comp_speed.reshape(2, N_PTS, comps // N_PTS)
    mask = sea_mask.reshape(2 * rows, GC).astype(jnp.float32)

    def block(item):
        field, speed_x, speed_y = item
        edge = jnp.zeros((field.shape[0], GC), jnp.float32)
        for step in range(SUBSTEPS):
            field = advect(field, speed_x, speed_y, mask, edge, edge)
        return field

    moved = lax.map(block, (stacked, speeds[0], speeds[1]))
    moved = moved.reshape(comps, 2 * points).T.reshape(2, held, N_PTS, comps)
    spectrum_next = jnp.transpose(moved, (0, 2, 1, 3)).reshape(2, points, comps)
    outs = []
    for g in range(2):
        stokes = jnp.dot(spectrum_next[g], stokes_kernel, precision=lax.Precision.HIGHEST, preferred_element_type=jnp.float32)
        ident = tile_owner[g, :, 0] * COLS + ocean_column[g]
        total = N_PTS * COLS
        drift_sum = jax.ops.segment_sum(stokes, ident, total)
        count = jax.ops.segment_sum(jnp.ones((points,), jnp.float32), ident, total)
        drift = (drift_sum / jnp.maximum(count, 1.0)[:, None]).T
        east_drift = drift[:LEVELS]
        north_drift = drift[LEVELS:]
        base = (jnp.arange(total, dtype=jnp.int32) // COLS * COLS)[:, None]
        near = neighbours[g] + base
        east_flow = velocity[g, 0]
        north_flow = velocity[g, 1]
        zeta = (north_flow[:, near[:, 0]] - north_flow[:, near[:, 1]]) - (east_flow[:, near[:, 2]] - east_flow[:, near[:, 3]])
        spin = coriolis[g][None, :]
        new_east = east_flow + 0.25 * (spin * north_flow + (spin + zeta) * north_drift)
        new_north = north_flow - 0.25 * (spin * east_flow + (spin + zeta) * east_drift)
        outs.append(jnp.stack([new_east, new_north]))
    return spectrum_next, jnp.stack(outs)
```

```python
import functools

import jax
import jax.numpy as jnp
from jax import lax
from jax.experimental import pallas as pl
from jax.experimental.pallas import tpu as pltpu
from jax.sharding import PartitionSpec as P


GC = 256
SUBSTEPS = 4
LANES = 128
SUBLANES = 8
SPLIT = (5, 4)
F32 = jnp.float32
BF16 = jnp.bfloat16

VMEM = pltpu.MemorySpace.VMEM
SMEM = pltpu.MemorySpace.SMEM


def round_up(value, unit):
    return -(-value // unit) * unit


def params():
    return pltpu.CompilerParams(vmem_limit_bytes=48 * 1024 * 1024)


def whole_vmem(count):
    return [pl.BlockSpec(memory_space=VMEM)] * count


def split_units(units):
    total = sum(SPLIT)
    edges = [0]
    for end in range(1, len(SPLIT) + 1):
        edges.append(max(edges[-1], round(sum(SPLIT[:end]) * units / total)))
    return [b - a for a, b in zip(edges[:-1], edges[1:]) if b > a]


def halves(value):
    high = value.astype(BF16)
    low = (value - high.astype(F32)).astype(BF16)
    return high, low


def unit_of(group):
    return 2 * SUBLANES * group


def relax_kernel(group, held, offset, spectrum, weights, out, rounded, turned):
    width = weights.shape[1]
    unit = unit_of(group)
    rounded[...] = spectrum[...].astype(BF16)
    for start in range(0, width, 256):
        size = min(256, width - start)
        mix = jnp.dot(
            rounded[...], weights[:, start : start + size], preferred_element_type=F32
        )
        local = spectrum[:, offset + start : offset + start + size]
        relaxed = local + 0.5 * local * jnp.tanh(mix)
        turned[start : start + size, :] = relaxed.T
    for start in range(0, width, unit):
        row = start // unit * SUBLANES
        for part in range(group):
            base = start + part * 2 * SUBLANES
            out[part, row : row + SUBLANES, :held] = turned[base : base + SUBLANES, :]
            out[part, row : row + SUBLANES, held:] = turned[
                base + SUBLANES : base + 2 * SUBLANES, :
            ]


def relax(spectrum, weights, group, first, units):
    held, comps = spectrum.shape
    unit = unit_of(group)
    offset, width = first * unit, units * unit
    block = (group, units * SUBLANES, 2 * held)
    return pl.pallas_call(
        functools.partial(relax_kernel, group, held, offset),
        grid=(1,),
        out_shape=jax.ShapeDtypeStruct(block, F32),
        in_specs=[
            pl.BlockSpec((held, comps), lambda i: (0, 0)),
            pl.BlockSpec((pl.Element(comps), pl.Element(width)), lambda i: (0, offset)),
        ],
        out_specs=pl.BlockSpec(block, lambda i: (0, 0, 0)),
        scratch_shapes=[pltpu.VMEM((held, comps), BF16), pltpu.VMEM((width, held), F32)],
        compiler_params=params(),
        name="relax",
    )(spectrum, weights)


def edge_rows(source, target, held, tall, first):
    base = 0 if first else held - tall
    for col in range(source.shape[0]):
        target[col, :, :tall] = source[col, :, base : base + tall]
        target[col, :, tall : 2 * tall] = source[col, :, held + base : held + base + tall]


def edge_kernel(held, tall, place, source, edge):
    rest = edge.shape[2] - 2 * tall
    if rest:
        edge[:, :, 2 * tall :] = jnp.zeros((edge.shape[0], edge.shape[1], rest), F32)

    @pl.when(place[1] == 0)
    def _():
        edge_rows(source, edge, held, tall, False)

    @pl.when(place[1] == 1)
    def _():
        edge_rows(source, edge, held, tall, True)


def edges_of(place, source, tall, edge_lanes):
    count, rows, width = source.shape
    return pl.pallas_call(
        functools.partial(edge_kernel, width // 2, tall),
        out_shape=jax.ShapeDtypeStruct((count, rows, edge_lanes), F32),
        in_specs=[pl.BlockSpec(memory_space=SMEM)] + whole_vmem(1),
        out_specs=pl.BlockSpec(memory_space=VMEM),
        compiler_params=params(),
        name="edge",
    )(place, source)


def pick_kernel(group, held, step, place, own, speeds, send):
    width = own.shape[2]
    lane = lax.broadcasted_iota(jnp.int32, (SUBLANES, width), 1)
    tiles = width // LANES

    def spread(part):
        return jnp.concatenate([speeds[0, part, 1]] * tiles, axis=1)

    forward = jnp.where(lane < held, spread(0), spread(1)) > 0.0
    spot = lax.rem(lane, step)

    @pl.when(place[0] == 1)
    def _():
        for col in range(SUBSTEPS):
            last = pltpu.roll(own[group - SUBSTEPS + col], 1, 1)
            last = jnp.where(spot == 0, 0.0, last)
            send[col] = jnp.where(forward, last, own[col])

    @pl.when(place[0] == 0)
    def _():
        for col in range(SUBSTEPS):
            first = pltpu.roll(own[col], width - 1, 1)
            first = jnp.where(spot == step - 1, 0.0, first)
            send[col] = jnp.where(forward, own[group - SUBSTEPS + col], first)


def pick(place, own, speeds, first, units, step):
    group, _, width = own.shape
    return pl.pallas_call(
        functools.partial(pick_kernel, group, width // 2, step),
        grid=(units,),
        out_shape=jax.ShapeDtypeStruct((SUBSTEPS, units * SUBLANES, width), F32),
        in_specs=[
            pl.BlockSpec(memory_space=SMEM),
            pl.BlockSpec((group, SUBLANES, width), lambda i: (0, i, 0)),
            pl.BlockSpec((1, 2, 2, SUBLANES, LANES), lambda i: (i + first, 0, 0, 0, 0)),
        ],
        out_specs=pl.BlockSpec((SUBSTEPS, SUBLANES, width), lambda i: (0, i, 0)),
        compiler_params=params(),
        name="pick",
    )(place, own, speeds)


def advect_kernel(held, tall, step, own, far, own_edge, far_edge, speeds, masks, out, field):
    group = own.shape[0]
    total = group + 2 * SUBSTEPS
    lanes = field.shape[2]
    tiles = lanes // LANES
    for part in range(2):
        base = part * held

        def fill(spot, source, col, edge, edge_col):
            if held + tall != lanes:
                field[spot] = jnp.zeros((SUBLANES, lanes), F32)
            rows = edge[edge_col, :, part * tall : (part + 1) * tall]
            field[spot, :, :held] = source[col, :, base : base + held]
            field[spot, :, held : held + tall] = rows
            if held + tall != lanes:
                field[spot, :, lanes - tall :] = rows

        for col in range(group):
            fill(SUBSTEPS + col, own, col, own_edge, col)
        for col in range(SUBSTEPS):
            fill(col, far, col, far_edge, col)
            field[SUBSTEPS + group + col] = field[col]

        def spread(one):
            return jnp.concatenate([one] * tiles, axis=1)

        along, across = speeds[0, part, 0], speeds[0, part, 1]
        centre = spread(1.0 - jnp.abs(along) - jnp.abs(across))
        up = spread(jnp.maximum(along, 0.0)) * masks[total : total + 1, :]
        down = spread(-jnp.minimum(along, 0.0)) * masks[total + 1 : total + 2, :]
        side = spread(jnp.abs(across))
        forward = spread(across) > 0.0
        for turn in range(SUBSTEPS):
            first = turn + 1
            end = total - 1 - turn
            before = field[first - 1]
            here = field[first]
            for spot in range(first, end):
                after = field[spot + 1]
                upwind = jnp.where(forward, before, after)
                value = (
                    centre * here
                    + up * pltpu.roll(here, step, 1)
                    + down * pltpu.roll(here, lanes - step, 1)
                    + side * upwind
                ) * masks[spot : spot + 1, :]
                if turn == SUBSTEPS - 1:
                    out[spot - SUBSTEPS, :, base : base + held] = value[:, :held]
                else:
                    field[spot] = value
                before = here
                here = after


def advect(own, far, own_edge, far_edge, speeds, masks, first, tall, step, lanes):
    group, _, width = own.shape
    rows = far.shape[1]
    edge_lanes = own_edge.shape[2]
    total = group + 2 * SUBSTEPS
    return pl.pallas_call(
        functools.partial(advect_kernel, width // 2, tall, step),
        grid=(rows // SUBLANES,),
        out_shape=jax.ShapeDtypeStruct((group, rows, width), F32),
        in_specs=[
            pl.BlockSpec((group, SUBLANES, width), lambda i: (0, i, 0)),
            pl.BlockSpec((SUBSTEPS, SUBLANES, width), lambda i: (0, i, 0)),
            pl.BlockSpec((group, SUBLANES, edge_lanes), lambda i: (0, i, 0)),
            pl.BlockSpec((SUBSTEPS, SUBLANES, edge_lanes), lambda i: (0, i, 0)),
            pl.BlockSpec((1, 2, 2, SUBLANES, LANES), lambda i: (i + first, 0, 0, 0, 0)),
            pl.BlockSpec((total + 2, lanes), lambda i: (0, 0)),
        ],
        out_specs=pl.BlockSpec((group, SUBLANES, width), lambda i: (0, i, 0)),
        scratch_shapes=[pltpu.VMEM((total, SUBLANES, lanes), F32)],
        compiler_params=params(),
        name="advect",
    )(own, far, own_edge, far_edge, speeds, masks)


def unpack(source, turned, base, held):
    group, rows, _ = source.shape
    for row in range(0, rows, SUBLANES):
        for part in range(group):
            start = base + row * 2 * group + part * 2 * SUBLANES
            piece = source[part, row : row + SUBLANES, :]
            turned[start : start + SUBLANES, :] = piece[:, :held]
            turned[start + SUBLANES : start + 2 * SUBLANES, :] = piece[:, held:]


def profile(source, kernel_turned, offset, turned, held):
    unpack(source, turned, 0, held)
    high, low = halves(turned[...])
    kernel_high, kernel_low = halves(kernel_turned[:, offset : offset + turned.shape[0]])
    return (
        jnp.dot(kernel_high, high, preferred_element_type=F32)
        + jnp.dot(kernel_low, high, preferred_element_type=F32)
        + jnp.dot(kernel_high, low, preferred_element_type=F32)
    )


def partial_kernel(held, offset, source, kernel_turned, out, turned):
    out[...] = profile(source, kernel_turned, offset, turned, held)


def partial_profile(source, kernel_turned, offset):
    group, half, width = source.shape
    held = width // 2
    return pl.pallas_call(
        functools.partial(partial_kernel, held, offset),
        out_shape=jax.ShapeDtypeStruct((kernel_turned.shape[0], held), F32),
        in_specs=whole_vmem(2),
        out_specs=pl.BlockSpec(memory_space=VMEM),
        scratch_shapes=[pltpu.VMEM((group * 2 * half, held), F32)],
        compiler_params=params(),
        name="profile",
    )(source, kernel_turned)


def place_kernel(held, offset, depth, rows, per_row, pieces, *refs):
    source, kernel_turned = refs[:2]
    earlier = refs[2 : 2 + pieces]
    slots, column, out, turned, payload = refs[2 + pieces :]
    total = profile(source, kernel_turned, offset, turned, held)
    for piece in earlier:
        total = total + piece[...]
    payload[...] = jnp.zeros((2 * LANES, held), BF16)
    high, low = halves(total)
    payload[:depth, :] = high
    payload[LANES : LANES + depth, :] = low
    place = lax.broadcasted_iota(jnp.int32, (SUBLANES, held), 0)
    tag = jnp.where(place == 0, jnp.broadcast_to(column[...], (SUBLANES, held)) + 1, 0)
    tag_high, tag_low = halves(tag.astype(F32))
    payload[depth : depth + SUBLANES, :] = tag_high
    payload[LANES + depth : LANES + depth + SUBLANES, :] = tag_low
    out[...] = jnp.zeros(out.shape, F32)
    for turn in range(per_row):
        wanted = lax.broadcasted_iota(jnp.int32, (rows, held), 0) + turn * rows
        chosen = jnp.where(wanted == slots[...], 1.0, 0.0).astype(BF16)
        both = lax.dot_general(
            chosen, payload[...], (((1,), (1,)), ((), ())), preferred_element_type=F32
        )
        value = both[:, :LANES] + both[:, LANES:]
        out[:, turn * depth : (turn + 1) * depth] = value[:, :depth]
        spot = per_row * depth + turn
        out[:, spot : spot + 1] = value[:, depth : depth + 1]


def place_rows(source, kernel_turned, offset, earlier, slots, column, tiles, per_row, lanes):
    group, half, width = source.shape
    held = width // 2
    depth = kernel_turned.shape[0]
    rows = tiles * SUBLANES
    return pl.pallas_call(
        functools.partial(place_kernel, held, offset, depth, rows, per_row, len(earlier)),
        out_shape=jax.ShapeDtypeStruct((rows, lanes), F32),
        in_specs=whole_vmem(4 + len(earlier)),
        out_specs=pl.BlockSpec(memory_space=VMEM),
        scratch_shapes=[
            pltpu.VMEM((group * 2 * half, held), F32),
            pltpu.VMEM((2 * LANES, held), BF16),
        ],
        compiler_params=params(),
        name="place",
    )(source, kernel_turned, *earlier, slots, column)


def restore_kernel(held, comps, count, *refs):
    sources = refs[:count]
    out, turned = refs[count:]
    base = 0
    for source in sources:
        unpack(source, turned, base, held)
        base += source.shape[0] * source.shape[1] * 2
    for start in range(0, comps, LANES):
        size = min(LANES, comps - start)
        out[0, :, start : start + size] = turned[start : start + size, :].T


def restore(sources, comps):
    held = sources[0].shape[2] // 2
    padded = sum(s.shape[0] * s.shape[1] * 2 for s in sources)
    return pl.pallas_call(
        functools.partial(restore_kernel, held, comps, len(sources)),
        out_shape=jax.ShapeDtypeStruct((1, held, comps), F32),
        in_specs=whole_vmem(len(sources)),
        out_specs=pl.BlockSpec(memory_space=VMEM),
        scratch_shapes=[pltpu.VMEM((padded, held), F32)],
        compiler_params=params(),
        name="restore",
    )(*sources)


def slot_kernel(rows, owner_down, owner_across, out):
    held = owner_across.shape[1]
    down = lax.broadcasted_iota(jnp.int32, (held, held), 0)
    across = lax.broadcasted_iota(jnp.int32, (held, held), 1)
    same = (owner_down[...] == owner_across[...]) & (down < across)
    rank = jnp.sum(jnp.where(same, 1.0, 0.0), axis=0, keepdims=True).astype(jnp.int32)
    turn = rank >> 3
    out[...] = turn * rows + owner_across[...] * SUBLANES + (rank - turn * SUBLANES)


def slots_of(owner, tiles):
    held = owner.shape[0]
    return pl.pallas_call(
        functools.partial(slot_kernel, tiles * SUBLANES),
        out_shape=jax.ShapeDtypeStruct((1, held), jnp.int32),
        in_specs=whole_vmem(2),
        out_specs=pl.BlockSpec(memory_space=VMEM),
        compiler_params=params(),
        name="slot",
    )(owner, owner.reshape(1, held))


def flow_kernel(near, spin_ref, velocity, out):
    east, north = velocity[0, 0], velocity[0, 1]
    columns = east.shape[1]
    spot = lax.broadcasted_iota(jnp.int32, (columns, columns), 0)

    def chooser(index):
        return jnp.where(spot == near[index : index + 1, :], 1.0, 0.0)

    def thirds(value):
        high = value.astype(BF16)
        rest = value - high.astype(F32)
        middle = rest.astype(BF16)
        return high, middle, (rest - middle.astype(F32)).astype(BF16)

    def taken(value, plus, minus):
        difference = (chooser(plus) - chooser(minus)).astype(BF16)
        parts = [jnp.dot(part, difference, preferred_element_type=F32) for part in thirds(value)]
        return parts[0] + parts[1] + parts[2]

    zeta = taken(north, 0, 1) - taken(east, 2, 3)
    spin = spin_ref[...]
    out[0] = east + 0.25 * (spin * north)
    out[1] = north - 0.25 * (spin * east)
    out[2] = 0.25 * (spin + zeta)


def flow(near, spin, velocity):
    _, _, levels, columns = velocity.shape
    return pl.pallas_call(
        flow_kernel,
        out_shape=jax.ShapeDtypeStruct((3, levels, columns), F32),
        in_specs=whole_vmem(3),
        out_specs=pl.BlockSpec(memory_space=VMEM),
        compiler_params=params(),
        name="flow",
    )(near, spin, velocity)


def drift_kernel(depth, per_row, received, base, out):
    rows, _ = received.shape
    columns = base.shape[2]
    levels = depth // 2
    spot = lax.broadcasted_iota(jnp.int32, (rows, columns), 1).astype(F32) + 1.0
    total = jnp.zeros((2 * LANES, columns), F32)
    count = jnp.zeros((1, columns), F32)
    for turn in range(per_row):
        at = per_row * depth + turn
        hit = jnp.where(received[:, at : at + 1] == spot, 1.0, 0.0)
        count = count + jnp.sum(hit, axis=0, keepdims=True)
        piece = received[:, turn * depth : (turn + 1) * depth]
        piece = jnp.concatenate([piece, jnp.zeros((rows, LANES - depth), F32)], axis=1)
        high, low = halves(piece.T)
        total = total + jnp.dot(
            jnp.concatenate([high, low], axis=0), hit.astype(BF16), preferred_element_type=F32
        )
    drift = (total[:depth] + total[LANES : LANES + depth]) / jnp.maximum(count, 1.0)
    out[0, 0] = base[0] + base[2] * drift[levels:]
    out[0, 1] = base[1] - base[2] * drift[:levels]


def drifted(received, base, depth, per_row):
    _, levels, columns = base.shape
    return pl.pallas_call(
        functools.partial(drift_kernel, depth, per_row),
        out_shape=jax.ShapeDtypeStruct((1, 2, levels, columns), F32),
        in_specs=whole_vmem(2),
        out_specs=pl.BlockSpec(memory_space=VMEM),
        compiler_params=params(),
        name="drift",
    )(received, base)


def coupled_step(
    spectrum,
    interaction,
    comp_speed,
    sea_mask,
    stokes_kernel,
    tile_owner,
    ocean_column,
    neighbours,
    coriolis,
    velocity,
):
    local = spectrum[0]
    held, comps = local.shape
    width = lax.axis_size("pts")
    group = width // 2
    step = GC // width
    rows = held // step
    tall = SUBSTEPS * step
    lanes = round_up(held + tall, LANES)
    edge_lanes = round_up(2 * tall, LANES)
    unit = 2 * SUBLANES * group
    units = -(-comps // unit)
    padded = units * unit
    if padded > comps:
        extra = padded - comps
        local = jnp.pad(local, ((0, 0), (0, extra)))
        interaction = jnp.pad(interaction, ((0, extra), (0, extra)))
        comp_speed = jnp.pad(comp_speed, ((0, 0), (0, extra)))
        stokes_kernel = jnp.pad(stokes_kernel, ((0, extra), (0, 0)))
    kernel_turned = stokes_kernel.T
    depth = kernel_turned.shape[0]

    grid_index = lax.axis_index("grid")
    index = lax.axis_index("pts")
    side = index // group
    member = index % group
    place = jnp.stack([side, grid_index]).astype(jnp.int32)
    teams = [list(range(group)), list(range(group, width))]
    across = [(i, (i + group) % width) for i in range(width)]
    other_grid = [(0, 1), (1, 0)]

    open_sea = jnp.pad(
        sea_mask.astype(F32).reshape(2, rows, GC), ((0, 0), (0, 0), (SUBSTEPS, group + SUBSTEPS))
    )
    open_sea = lax.dynamic_slice_in_dim(open_sea, side * group, GC, 2)
    total = group + 2 * SUBSTEPS
    open_sea = open_sea.reshape(2, rows, step, width)[:, :, :, :total]
    open_sea = jnp.transpose(open_sea, (0, 3, 1, 2)).reshape(2, total, held)
    mine = jnp.where(grid_index == 0, open_sea[0], open_sea[1])
    edge_mask = jnp.where(grid_index == 0, open_sea[1][:, :tall], open_sea[0][:, held - tall :])
    if held + tall == lanes:
        masks = jnp.concatenate([mine, edge_mask], axis=1)
    else:
        gap = jnp.zeros((total, lanes - held - 2 * tall), F32)
        masks = jnp.concatenate([mine, edge_mask, gap, edge_mask], axis=1)
    lane = jnp.arange(lanes, dtype=jnp.int32)
    up_open = 1.0 - ((grid_index == 0) & (lane < step)).astype(F32)
    down_open = 1.0 - (
        (grid_index == 1) & (lane >= held - step) & (lane < held)
    ).astype(F32)
    masks = jnp.concatenate([masks, up_open[None], down_open[None]], axis=0)
    slots = slots_of(tile_owner[0], width)
    base = flow(neighbours[0].T, coriolis, velocity)

    speeds = comp_speed.reshape(2, units, group, 2, SUBLANES)
    speeds = lax.dynamic_index_in_dim(speeds, member, 2, keepdims=False)
    speeds = jnp.transpose(speeds, (1, 2, 0, 3))
    speeds = jnp.broadcast_to(speeds[..., None], speeds.shape + (LANES,))
    speeds, masks, kernel_turned = lax.optimization_barrier((speeds, masks, kernel_turned))

    team_exchange = functools.partial(
        lax.all_to_all,
        axis_name="pts",
        split_axis=0,
        concat_axis=0,
        tiled=True,
        axis_index_groups=teams,
    )
    plan = []
    first = 0
    for amount in split_units(units):
        plan.append((first, amount))
        first += amount
    count = len(plan)
    sent = []
    for first, amount in plan:
        sent.append(relax(local, interaction, group, first, amount))

    returned = []
    for number, (first, amount) in enumerate(plan):
        own = team_exchange(sent[number])
        send = pick(place, own, speeds, first, amount, step)
        if number + 1 < count:
            send, sent[number + 1] = lax.optimization_barrier((send, sent[number + 1]))
        far = lax.ppermute(send, "pts", across)
        edge = edges_of(place, own, tall, edge_lanes)
        own_edge = lax.ppermute(edge, "grid", other_grid)
        far_edge = edges_of(place, far, tall, edge_lanes)
        far_edge = lax.ppermute(far_edge, "grid", other_grid)
        moved = advect(own, far, own_edge, far_edge, speeds, masks, first, tall, step, lanes)
        returned.append(team_exchange(moved))

    capacity = 2 * held // width
    per_row = -(-capacity // SUBLANES)
    row_lanes = round_up(per_row * (depth + 1), LANES)

    earlier = [
        partial_profile(returned[n], kernel_turned, plan[n][0] * unit) for n in range(count - 1)
    ]
    buffer = place_rows(
        returned[-1],
        kernel_turned,
        plan[-1][0] * unit,
        earlier,
        slots,
        ocean_column,
        width,
        per_row,
        row_lanes,
    )
    received = lax.all_to_all(
        buffer.reshape(width, SUBLANES, row_lanes), "pts", split_axis=0, concat_axis=0, tiled=True
    )
    spectrum_next = restore(returned, comps)
    velocity_next = drifted(
        received.reshape(width * SUBLANES, row_lanes), base, depth, per_row
    )
    return (spectrum_next, velocity_next)


def solution(mesh):
    placed = (
        P("grid", "pts", None),
        P(),
        P(),
        P(),
        P(),
        P("grid", "pts", None),
        P("grid", "pts"),
        P("grid", "pts", None),
        P("grid", "pts"),
        P("grid", None, None, "pts"),
    )
    return jax.shard_map(
        coupled_step,
        mesh=mesh,
        in_specs=placed,
        out_specs=(P("grid", "pts", None), P("grid", None, None, "pts")),
        check_vma=False,
    )
```
